32 devices in a mesh: ctx: 8 (over z, y), head: 4 (over x, core).
Axes of the slice: x: 2, y: 2, z: 4, core: 2. Of those that a mesh axis runs over, the one named last changes fastest.
Arguments:
- hidden: bfloat16 [256, 4096], P('head', 'ctx'), may hold values from -60 to 60
- norm_gain: float32 [4096], P('ctx'), may hold values from 0.1 to 1.9
- w_qkv: bfloat16 [4096, 6144], P('ctx'), may hold values from -0.09375 to 0.09375
- positions: int32 [256], replicated, may hold values from 0 to 510, as said below
- cache_keys: bfloat16 [32768, 1024], P('ctx', 'head'), may hold values from -450 to 450
- cache_values: bfloat16 [32768, 1024], P('ctx', 'head'), may hold values from -6 to 6
- key_counts: int32 [8], P('ctx'), may hold values from 2048 to 4096, as said below
- w_out: bfloat16 [4096, 4096], P('head', 'ctx'), may hold values from -6 to 6
Outputs:
- attn_proj: bfloat16 [256, 4096], P('head', 'ctx')
The draws below stay inside these ranges and needn't reach their ends.
Inputs may be any that keep to these rules, and one draw needn't show every extreme that they name: Rows of the question have positions that start at 0 and rise by 1 to 3 from one row to the next; the last row stands at position 510; cached keys were rotated at positions relative to the same anchor. In context block c only the first key_counts[c] of its 4096 rows are valid; in every draw some block is full.
All inputs are finite; a program needn't handle non-finite values.
Results may differ from the reference program's by a relative error of at most 0.0055.
The reference program's roundings to bfloat16 on the way count: a program that leaves them out, or rounds other values in their place, can miss the bound.
Values may be sent and summed in bfloat16 or wider, within the bound.
A program may use at most 64 MiB of HBM per device.

```python
import math
import jax
import jax.numpy as jnp
from jax import lax

D = 4096
HEADS = 32
KV_HEADS = 8
HEAD_DIM = 128
KEYS_DEV = 4096
TQ = 256
KEYS = 32768
QKV = 6144
N_CTX = 8


def draw_hidden(key, part):
    col_pos = jnp.arange(D, dtype=jnp.float32) / (D - 1)
    base_vals = jnp.clip(jax.random.normal(key, (TQ, D), jnp.float32), -5.0, 5.0)
    values_out = base_vals * (0.6 * 3.0 ** col_pos)[None, :]
    return values_out.astype(jnp.bfloat16)


def draw_positions(key, part):
    pair_gaps = jax.random.randint(key, ((TQ - 2) // 2,), 1, 4)
    paired = jnp.stack([pair_gaps, 4 - pair_gaps], axis=1).reshape(-1)
    gap_sizes = jnp.concatenate([paired, jnp.full((1,), 2, jnp.int32)])
    return jnp.concatenate([jnp.zeros((1,), jnp.int32), jnp.cumsum(gap_sizes).astype(jnp.int32)]).astype(jnp.int32)


def draw_key_counts(key, part):
    key_one, key_two = jax.random.split(key)
    counts_out = jax.random.randint(key_one, (N_CTX,), KEYS_DEV // 2, KEYS_DEV + 1)
    full_group = jax.random.randint(key_two, (), 0, N_CTX)
    return counts_out.at[full_group].set(KEYS_DEV).astype(jnp.int32)


def draw_cache_keys(key, part):
    width_all = KV_HEADS * HEAD_DIM
    key_one = jax.random.fold_in(key, 0)
    base_vals = jnp.clip(jax.random.normal(key_one, (KEYS_DEV * N_CTX, width_all), jnp.float32), -6.0, 6.0)
    return base_vals.astype(jnp.bfloat16)


def steps_of(own_key, extent, cuts, low, high):
    gain, own = 1.0, jax.random.fold_in(own_key, 6)
    for dim, parts in cuts:
        heights = jnp.exp(jax.random.uniform(jax.random.fold_in(own, dim), (parts,), jnp.float32, low / len(cuts), high / len(cuts)))
        gain = gain * jnp.repeat(heights, extent[dim] // parts).reshape([-1 if axis == dim else 1 for axis in range(len(extent))])
    return gain


def scatter_about(rng, extent, width, bound, pieces=(), kind=jnp.bfloat16):
    entries = width * jax.random.normal(rng, extent, jnp.float32)
    if pieces:
        entries = entries * steps_of(rng, extent, pieces, -0.22, 0.18)
    return jnp.clip(entries, -bound, bound).astype(kind)


def setup_inputs(seed: int = 0) -> dict:
    key_of = jax.random.split(jax.random.key(seed), 9)
    return {
        "hidden": draw_hidden(jax.random.fold_in(key_of[8], 71), 0),
        "norm_gain": jnp.clip(1.0 + 0.18 * jax.random.normal(key_of[1], (D,), jnp.float32), 0.1, 1.9),
        "w_qkv": scatter_about(key_of[2], (D, QKV), D ** -0.5, 0.09375, ((0, 8),)),
        "positions": draw_positions(jax.random.fold_in(key_of[8], 71), 0),
        "cache_keys": draw_cache_keys(jax.random.fold_in(key_of[8], 71), 0),
        "cache_values": scatter_about(key_of[5], (KEYS, KV_HEADS * HEAD_DIM), 1.0, 6.0, ((0, 8), (1, 4))),
        "key_counts": draw_key_counts(jax.random.fold_in(key_of[8], 71), 0),
        "w_out": scatter_about(key_of[7], (HEADS * HEAD_DIM, D), 1.5, 6.0, ((0, 4), (1, 8))),
    }


NEG_FILL = -1e+30

def rotate(values_in, positions_in):
    half_dim = values_in.shape[-1] // 2
    frequency = 500000.0 ** (-(jnp.arange(half_dim, dtype=jnp.float32) * 2.0 / values_in.shape[-1]))
    angles = positions_in.astype(jnp.float32)[:, None] * frequency[None, :]
    angles = angles.reshape((angles.shape[0],) + (1,) * (values_in.ndim - 2) + (half_dim,))
    cosine = jnp.cos(angles)
    sine_val = jnp.sin(angles)
    first_half = values_in[..., :half_dim]
    second = values_in[..., half_dim:]
    return jnp.concatenate([first_half * cosine - second * sine_val, second * cosine + first_half * sine_val], axis=-1)

def attend(query_block, key_block, value_block, new_keys, new_values, cache_mask, self_mask):
    score_scale = 1.0 / math.sqrt(query_block.shape[-1])
    query_f = query_block.astype(jnp.float32)
    score_cache = jnp.einsum('tagh,kah->tagk', query_f, key_block.astype(jnp.float32)) * score_scale
    score_self = jnp.einsum('tagh,uah->tagu', query_f, new_keys.astype(jnp.float32)) * score_scale
    score_cache = jnp.where(cache_mask[None, None, None, :], score_cache, NEG_FILL)
    score_self = jnp.where(self_mask[:, None, None, :], score_self, NEG_FILL)
    row_max = jnp.maximum(lax.optimization_barrier(jnp.max(score_cache, axis=-1)), lax.optimization_barrier(jnp.max(score_self, axis=-1)))
    exp_cache = jnp.exp(score_cache - row_max[..., None]).astype(jnp.bfloat16)
    exp_self = jnp.exp(score_self - row_max[..., None]).astype(jnp.bfloat16)
    totals = lax.optimization_barrier(jnp.sum(exp_cache.astype(jnp.float32), axis=-1)) + lax.optimization_barrier(jnp.sum(exp_self.astype(jnp.float32), axis=-1))
    weighted = jnp.einsum('tagk,kah->tagh', exp_cache.astype(jnp.float32), value_block.astype(jnp.float32))
    weighted = weighted + jnp.einsum('tagu,uah->tagh', exp_self.astype(jnp.float32), new_values.astype(jnp.float32))
    return (row_max, totals, weighted)

def reference(hidden, norm_gain, w_qkv, positions, cache_keys, cache_values, key_counts, w_out):
    group_size = HEADS // KV_HEADS
    hidden_f = hidden.astype(jnp.float32)
    inv_rms = lax.rsqrt(lax.optimization_barrier(jnp.mean(hidden_f * hidden_f, axis=1)) + 1e-05)
    scaled = (hidden_f * norm_gain[None, :]).astype(jnp.bfloat16)
    mixed_cols = jnp.dot(scaled, w_qkv, preferred_element_type=jnp.float32) * inv_rms[:, None]
    mixed_cols = mixed_cols.reshape(TQ, KV_HEADS, group_size + 2, HEAD_DIM)
    turned = rotate(mixed_cols[:, :, :group_size + 1], positions)
    rotated = jnp.concatenate([turned, mixed_cols[:, :, group_size + 1:]], axis=2).astype(jnp.bfloat16)
    queries = rotated[:, :, :group_size]
    new_keys = rotated[:, :, group_size]
    new_values = rotated[:, :, group_size + 1]
    keys_all = cache_keys.reshape(N_CTX, KEYS_DEV, KV_HEADS, HEAD_DIM)
    values_all = cache_values.reshape(N_CTX, KEYS_DEV, KV_HEADS, HEAD_DIM)
    block_rows = math.gcd(TQ, 128)
    block_count = TQ // block_rows
    query_blocks = queries.reshape(block_count, block_rows, KV_HEADS, group_size, HEAD_DIM)
    block_starts = jnp.arange(block_count, dtype=jnp.int32) * block_rows

    def one_group(state_in, inputs):
        key_block, value_block, valid_count, group_index = inputs
        cache_mask = jnp.arange(KEYS_DEV, dtype=jnp.int32) < valid_count

        def one_block(block_args):
            query_block, row_start = block_args
            rows_here = row_start + jnp.arange(block_rows, dtype=jnp.int32)
            self_mask = (jnp.arange(TQ, dtype=jnp.int32)[None, :] <= rows_here[:, None]) & (group_index == 0)
            return attend(query_block, key_block, value_block, new_keys, new_values, cache_mask, self_mask)
        part_max, part_sum, part_out = lax.map(one_block, (query_blocks, block_starts))
        part_max = part_max.reshape(TQ, KV_HEADS, group_size)
        part_sum = part_sum.reshape(TQ, KV_HEADS, group_size)
        part_out = part_out.reshape(TQ, KV_HEADS, group_size, HEAD_DIM)
        max_a, sum_a, out_a = state_in
        joined_max = jnp.maximum(max_a, part_max)
        weight_a = jnp.exp(max_a - joined_max)
        weight_b = jnp.exp(part_max - joined_max)
        joined_sum = sum_a * weight_a + part_sum * weight_b
        joined_out = out_a * weight_a[..., None] + part_out * weight_b[..., None]
        return ((joined_max, joined_sum, joined_out), None)
    start_state = (jnp.full((TQ, KV_HEADS, group_size), NEG_FILL, jnp.float32), jnp.zeros((TQ, KV_HEADS, group_size), jnp.float32), jnp.zeros((TQ, KV_HEADS, group_size, HEAD_DIM), jnp.float32))
    group_ids = jnp.arange(N_CTX, dtype=jnp.int32)
    final_state, _ = lax.scan(one_group, start_state, (keys_all, values_all, key_counts, group_ids))
    final_max, final_sum, final_out = final_state
    attended = (final_out / final_sum[..., None]).astype(jnp.bfloat16).reshape(TQ, HEADS * HEAD_DIM)
    return jnp.dot(attended, w_out, preferred_element_type=jnp.float32).astype(jnp.bfloat16)
```

```python
import functools
import math

import jax
import jax.numpy as jnp
from jax import lax
from jax.experimental import pallas as pl
from jax.experimental.pallas import tpu as pltpu
from jax.sharding import PartitionSpec as P

HEADS = 32
KV_HEADS = 8
HEAD_DIM = 128
GROUP = HEADS // KV_HEADS
SLOTS = GROUP + 2
NEG_FILL = -1e30
MESH = pl.DeviceIdType.MESH
F32 = jnp.float32
BF16 = jnp.bfloat16


def rows_at(index, size):
    return pl.ds(pl.multiple_of(index * size, size), size)


def kernel(
    n_ctx, n_head, fast, slow,
    hid, gain, cosine, sine, count, w_qkv, keys, values, w_out,
    out,
    hid_all, w_buf, k_buf, v_buf, wo_buf, ss_own, ss_in, part,
    fast_in, slow_out, slow_in, q_all, scores, causal, o_own, o_send, st_own,
    of_in, sf_in, os_out, ss_out, os_in, sst_in, a_all, y_send, y_in,
    local_sem, hid_sem, sq_sem, rs1_sem, rs2_sem, ag1_sem, of_sem, sf_sem, os_sem, sst_sem, ag2_sem, y_sem,
):
    c = lax.axis_index("ctx")
    h = lax.axis_index("head")
    z = c // fast
    y = c % fast
    rows = hid.shape[0]
    total = rows * n_head
    own = total // n_ctx
    depth = hid.shape[1]
    width = w_buf.shape[1]
    groups = k_buf.shape[0]
    key_rows = keys.shape[0]
    heads = groups * GROUP
    wide = heads * HEAD_DIM
    sends = []

    def send(src, dst, sems, slot, axis, peer):
        copy = pltpu.make_async_remote_copy(
            src_ref=src, dst_ref=dst,
            send_sem=sems.at[(0,) + slot], recv_sem=sems.at[(1,) + slot],
            device_id={axis: peer}, device_id_type=MESH,
        )
        copy.start()
        sends.append(copy)
        return copy

    locals_ = [
        pltpu.make_async_copy(w_qkv.at[:, pl.ds(pl.multiple_of(h * width, width), width)], w_buf, local_sem.at[0])
    ]
    for g in range(groups):
        cols = pl.ds(g * HEAD_DIM, HEAD_DIM)
        locals_.append(
            pltpu.make_async_copy(keys.at[:, cols], k_buf.at[g, pl.ds(0, key_rows)], local_sem.at[2 + 2 * g])
        )
        locals_.append(
            pltpu.make_async_copy(
                values.at[:, cols], v_buf.at[g, pl.ds(0, key_rows), pl.ds(0, HEAD_DIM)], local_sem.at[3 + 2 * g]
            )
        )
    locals_.append(pltpu.make_async_copy(w_out, wo_buf, local_sem.at[1]))
    for copy in locals_:
        copy.start()

    barrier = pltpu.get_barrier_semaphore()
    for k in range(1, n_head):
        pl.semaphore_signal(barrier, inc=1, device_id={"head": (h + k) % n_head}, device_id_type=MESH)
    for k in range(1, n_ctx):
        pl.semaphore_signal(barrier, inc=1, device_id={"ctx": (c + k) % n_ctx}, device_id_type=MESH)
    pl.semaphore_wait(barrier, n_head + n_ctx - 2)

    my_rows = rows_at(h, rows)
    gathers = [
        send(hid, hid_all.at[my_rows], hid_sem, (k - 1,), "head", (h + k) % n_head) for k in range(1, n_head)
    ]
    hid_all[my_rows, :] = hid[...]
    v_buf[:, :, HEAD_DIM:] = jnp.ones((groups, key_rows + total, HEAD_DIM), BF16)
    row_ids = lax.broadcasted_iota(jnp.int32, (total, total), 0)
    col_ids = lax.broadcasted_iota(jnp.int32, (total, total), 1)
    causal[...] = jnp.where(col_ids <= row_ids, jnp.where(c == 0, 0.0, NEG_FILL), NEG_FILL)
    for copy in gathers:
        copy.wait_recv()

    features = hid_all[...].astype(F32)
    scaled = (features * gain[...]).astype(BF16)
    squares = features * features
    high = squares.astype(BF16)
    low = (squares - high.astype(F32)).astype(BF16)
    ones = jnp.ones((8, depth), BF16)
    contract = (((1,), (1,)), ((), ()))
    ss_own[...] = lax.dot_general(ones, high, contract, preferred_element_type=F32) + lax.dot_general(
        ones, low, contract, preferred_element_type=F32
    )
    squares_in = [
        send(ss_own, ss_in.at[k - 1], sq_sem, (k - 1,), "ctx", (c + k) % n_ctx) for k in range(1, n_ctx)
    ]
    locals_[0].wait()
    step = width // 3
    for j in range(3):
        cols = pl.ds(j * step, step)
        block = jnp.dot(scaled, w_buf[:, cols], preferred_element_type=F32)
        part[:, cols] = block

    firsts = {}
    for k in list(range(1, slow)) + [0]:
        for j in range(1, fast):
            peer_y = (y + j) % fast
            peer_z = (z + k) % slow
            firsts[j, k] = send(
                part.at[rows_at(peer_z * fast + peer_y, own)], fast_in.at[j - 1, k],
                rs1_sem, (j - 1, k), "ctx", z * fast + peer_y,
            )
    seconds = []
    for k in list(range(1, slow)) + [0]:
        chunk = (z + k) % slow
        block = part[rows_at(chunk * fast + y, own), :]
        for j in range(1, fast):
            firsts[j, k].wait_recv()
            block = block + fast_in[j - 1, k]
        if k:
            slow_out[k - 1] = block
            seconds.append(
                send(slow_out.at[k - 1], slow_in.at[k - 1], rs2_sem, (k - 1,), "ctx", chunk * fast + y)
            )
    mixed = block
    for copy in squares_in:
        copy.wait_recv()
    square_total = ss_own[0:1, :]
    for k in range(1, n_ctx):
        square_total = square_total + ss_in[k - 1, 0:1, :]
    picked = lax.broadcasted_iota(jnp.int32, (own, total), 1) == (
        lax.broadcasted_iota(jnp.int32, (own, total), 0) + c * own
    )
    square_rows = jnp.sum(jnp.where(picked, square_total, 0.0), axis=1, keepdims=True)
    inv_rms = lax.rsqrt(square_rows / (depth * n_ctx) + 1e-05)
    for k in range(1, slow):
        seconds[k - 1].wait_recv()
        mixed = mixed + slow_in[k - 1]
    mixed = mixed * inv_rms
    my_chunk = rows_at(c, own)
    for slot in range(groups * SLOTS):
        cols = pl.ds(slot * HEAD_DIM, HEAD_DIM)
        entry = mixed[:, slot * HEAD_DIM : (slot + 1) * HEAD_DIM]
        if slot % SLOTS <= GROUP:
            entry = entry * cosine[...] + pltpu.roll(entry, HEAD_DIM // 2, 1) * sine[...]
        q_all[my_chunk, cols] = entry.astype(BF16)

    def gather_chunks(ref, sems):
        across = [
            send(ref.at[my_chunk], ref.at[my_chunk], sems, (0, k), "ctx", ((z + k) % slow) * fast + y)
            for k in range(1, slow)
        ]
        along = [
            send(ref.at[my_chunk], ref.at[my_chunk], sems, (j, 0), "ctx", z * fast + (y + j) % fast)
            for j in range(1, fast)
        ]
        for k in range(1, slow):
            across[k - 1].wait_recv()
            block_rows = rows_at(((z + slow - k) % slow) * fast + y, own)
            for j in range(1, fast):
                along.append(
                    send(ref.at[block_rows], ref.at[block_rows], sems, (j, k), "ctx", z * fast + (y + j) % fast)
                )
        for copy in along:
            copy.wait_recv()

    gather_chunks(q_all, ag1_sem)

    for copy in locals_[1:-1]:
        copy.wait()
    for g in range(groups):
        base = (g * SLOTS + GROUP) * HEAD_DIM
        k_buf[g, pl.ds(key_rows, total), :] = q_all[:, pl.ds(base, HEAD_DIM)]
        v_buf[g, pl.ds(key_rows, total), pl.ds(0, HEAD_DIM)] = q_all[:, pl.ds(base + HEAD_DIM, HEAD_DIM)]
    rate = math.log2(math.e) / math.sqrt(HEAD_DIM)
    key_step = 512
    valid = count[0]
    lanes = lax.broadcasted_iota(jnp.int32, (total, 128), 1)

    def one_head(i, stats):
        g = i // GROUP
        query = q_all[:, pl.ds(pl.multiple_of((g * SLOTS + i % GROUP) * HEAD_DIM, HEAD_DIM), HEAD_DIM)]
        spans = [(start, key_step) for start in range(0, key_rows, key_step)] + [(key_rows, total)]
        top = None
        for start, size in spans:
            score = lax.dot_general(
                query, k_buf[g, pl.ds(start, size), :], contract, preferred_element_type=F32
            )
            if start == key_rows:
                score = score + causal[...]
            elif start + size > key_rows // 2:
                ids = start + lax.broadcasted_iota(jnp.int32, (1, size), 1)
                score = score + jnp.where(ids < valid, 0.0, NEG_FILL)
            scores[:, pl.ds(start, size)] = score
            for lane in range(0, size, 128):
                piece = score[:, lane : lane + 128]
                top = piece if top is None else jnp.maximum(top, piece)
        peak = jnp.max(top, axis=1, keepdims=True)
        sums = jnp.zeros((total, 2 * HEAD_DIM), F32)
        for start, size in spans:
            weight = jnp.exp2((scores[:, pl.ds(start, size)] - peak) * rate).astype(BF16)
            sums = sums + jnp.dot(weight, v_buf[g, pl.ds(start, size), :], preferred_element_type=F32)
        o_cols = pl.ds(pl.multiple_of(i * HEAD_DIM, HEAD_DIM), HEAD_DIM)
        o_own[:, o_cols] = sums[:, :HEAD_DIM]
        o_send[:, o_cols] = sums[:, :HEAD_DIM].astype(BF16)
        stats = jnp.where(lanes == i, peak, stats)
        return jnp.where(lanes == 64 + i, sums[:, HEAD_DIM:], stats)

    st_own[...] = lax.fori_loop(0, heads, one_head, jnp.zeros((total, 128), F32))

    own_lanes = lax.broadcasted_iota(jnp.int32, (own, 128), 1)

    def merge(parts):
        top = parts[0][1]
        for _, stat in parts[1:]:
            top = jnp.maximum(top, stat)
        factors = [jnp.exp2((stat - top) * rate) for _, stat in parts]
        sums = None
        for (_, stat), factor in zip(parts, factors):
            term = stat * pltpu.roll(factor, 64, 1)
            sums = term if sums is None else sums + term
        outs = []
        for i in range(heads):
            acc = None
            for (load, _), factor in zip(parts, factors):
                term = load(i) * factor[:, i : i + 1]
                acc = term if acc is None else acc + term
            outs.append(acc)
        return outs, jnp.where(own_lanes < 64, top, sums)

    def cols_of(ref, *index):
        return lambda i: ref[index + (slice(None), pl.ds(i * HEAD_DIM, HEAD_DIM))].astype(F32)

    firsts = {}
    for k in list(range(1, slow)) + [0]:
        for j in range(1, fast):
            peer_y = (y + j) % fast
            chunk_rows = rows_at(((z + k) % slow) * fast + peer_y, own)
            firsts[j, k] = (
                send(st_own.at[chunk_rows], sf_in.at[j - 1, k], sf_sem, (j - 1, k), "ctx", z * fast + peer_y),
                send(o_send.at[chunk_rows], of_in.at[j - 1, k], of_sem, (j - 1, k), "ctx", z * fast + peer_y),
            )
    seconds = []
    for k in list(range(1, slow)) + [0]:
        chunk = (z + k) % slow
        chunk_rows = rows_at(chunk * fast + y, own)
        parts = [
            (lambda i, at=chunk_rows: o_own[at, pl.ds(i * HEAD_DIM, HEAD_DIM)], st_own[chunk_rows, :])
        ]
        for j in range(1, fast):
            for copy in firsts[j, k]:
                copy.wait_recv()
            parts.append((cols_of(of_in, j - 1, k), sf_in[j - 1, k]))
        outs, stat = merge(parts)
        if k:
            ss_out[k - 1] = stat
            for i in range(heads):
                os_out[k - 1, :, pl.ds(i * HEAD_DIM, HEAD_DIM)] = outs[i].astype(BF16)
            seconds.append((
                send(ss_out.at[k - 1], sst_in.at[k - 1], sst_sem, (k - 1,), "ctx", chunk * fast + y),
                send(os_out.at[k - 1], os_in.at[k - 1], os_sem, (k - 1,), "ctx", chunk * fast + y),
            ))
    parts = [(lambda i: outs[i], stat)]
    for k in range(1, slow):
        for copy in seconds[k - 1]:
            copy.wait_recv()
        parts.append((cols_of(os_in, k - 1), sst_in[k - 1]))
    final, stat = merge(parts)
    for i in range(heads):
        a_all[my_chunk, pl.ds(i * HEAD_DIM, HEAD_DIM)] = (final[i] / stat[:, 64 + i : 65 + i]).astype(BF16)
    gather_chunks(a_all, ag2_sem)

    locals_[-1].wait()
    mine = jnp.dot(a_all[my_rows, :], wo_buf[...], preferred_element_type=F32)
    y_send[...] = jnp.dot(a_all[...], wo_buf[...], preferred_element_type=F32).astype(BF16)
    shares = [
        send(y_send.at[rows_at((h + k) % n_head, rows)], y_in.at[k - 1], y_sem, (k - 1,), "head", (h + k) % n_head)
        for k in range(1, n_head)
    ]
    for k in range(1, n_head):
        shares[k - 1].wait_recv()
        mine = mine + y_in[k - 1].astype(F32)
    out[...] = mine.astype(out.dtype)
    for copy in sends:
        copy.wait_send()


def per_device(n_ctx, n_head, hidden, norm_gain, w_qkv, positions, cache_keys, cache_values, key_counts, w_out):
    fast = 2 if n_ctx <= 8 else 8
    slow = n_ctx // fast
    rows, depth = hidden.shape
    total = rows * n_head
    own = total // n_ctx
    groups = KV_HEADS // n_head
    width = groups * SLOTS * HEAD_DIM
    wide = groups * GROUP * HEAD_DIM
    key_rows = cache_keys.shape[0]
    half = HEAD_DIM // 2
    frequency = 500000.0 ** (-(jnp.arange(half, dtype=F32) * 2.0 / HEAD_DIM))
    mine = lax.dynamic_slice_in_dim(positions, lax.axis_index("ctx") * own, own)
    angles = mine.astype(F32)[:, None] * frequency[None, :]
    cosine, sine = jnp.cos(angles), jnp.sin(angles)
    cosine = jnp.concatenate([cosine, cosine], axis=1)
    sine = jnp.concatenate([-sine, sine], axis=1)
    vmem = pl.BlockSpec(memory_space=pltpu.VMEM)
    hbm = pl.BlockSpec(memory_space=pl.ANY)
    dma = pltpu.SemaphoreType.DMA
    return pl.pallas_call(
        functools.partial(kernel, n_ctx, n_head, fast, slow),
        out_shape=jax.ShapeDtypeStruct((rows, w_out.shape[1]), BF16),
        in_specs=[vmem, vmem, vmem, vmem, pl.BlockSpec(memory_space=pltpu.SMEM), hbm, hbm, hbm, hbm],
        out_specs=vmem,
        scratch_shapes=[
            pltpu.VMEM((total, depth), BF16),
            pltpu.VMEM((depth, width), BF16),
            pltpu.VMEM((groups, key_rows + total, HEAD_DIM), BF16),
            pltpu.VMEM((groups, key_rows + total, 2 * HEAD_DIM), BF16),
            pltpu.VMEM(w_out.shape, BF16),
            pltpu.VMEM((8, total), F32),
            pltpu.VMEM((n_ctx - 1, 8, total), F32),
            pltpu.VMEM((total, width), F32),
            pltpu.VMEM((fast - 1, slow, own, width), F32),
            pltpu.VMEM((slow - 1, own, width), F32),
            pltpu.VMEM((slow - 1, own, width), F32),
            pltpu.VMEM((total, width), BF16),
            pltpu.VMEM((total, key_rows + total), F32),
            pltpu.VMEM((total, total), F32),
            pltpu.VMEM((total, wide), F32),
            pltpu.VMEM((total, wide), BF16),
            pltpu.VMEM((total, 128), F32),
            pltpu.VMEM((fast - 1, slow, own, wide), BF16),
            pltpu.VMEM((fast - 1, slow, own, 128), F32),
            pltpu.VMEM((slow - 1, own, wide), BF16),
            pltpu.VMEM((slow - 1, own, 128), F32),
            pltpu.VMEM((slow - 1, own, wide), BF16),
            pltpu.VMEM((slow - 1, own, 128), F32),
            pltpu.VMEM((total, wide), BF16),
            pltpu.VMEM((total, w_out.shape[1]), BF16),
            pltpu.VMEM((n_head - 1, rows, w_out.shape[1]), BF16),
            dma((2 + 2 * groups,)),
            dma((2, n_head - 1)),
            dma((2, n_ctx - 1)),
            dma((2, fast - 1, slow)),
            dma((2, slow - 1)),
            dma((2, fast, slow)),
            dma((2, fast - 1, slow)),
            dma((2, fast - 1, slow)),
            dma((2, slow - 1)),
            dma((2, slow - 1)),
            dma((2, fast, slow)),
            dma((2, n_head - 1)),
        ],
        compiler_params=pltpu.CompilerParams(
            collective_id=0, has_side_effects=True, vmem_limit_bytes=60 * 1024 * 1024
        ),
    )(hidden, norm_gain.reshape(1, depth), cosine, sine, key_counts, w_qkv, cache_keys, cache_values, w_out)


def solution(mesh):
    return jax.shard_map(
        functools.partial(per_device, mesh.shape["ctx"], mesh.shape["head"]),
        mesh=mesh,
        in_specs=(
            P("head", "ctx"),
            P("ctx"),
            P("ctx", None),
            P(),
            P("ctx", "head"),
            P("ctx", "head"),
            P("ctx"),
            P("head", "ctx"),
        ),
        out_specs=P("head", "ctx"),
        check_vma=False,
    )
```

```python
import functools
import math

import jax
import jax.numpy as jnp
import numpy as np
from jax import lax
from jax.experimental import pallas as pl
from jax.experimental.pallas import tpu as pltpu
from jax.sharding import PartitionSpec as P

HEADS = 32
KV_HEADS = 8
HEAD_DIM = 128
GROUP = HEADS // KV_HEADS
SLOTS = GROUP + 2
NEG_FILL = -1e30
MESH = pl.DeviceIdType.MESH
F32 = jnp.float32
BF16 = jnp.bfloat16


def rows_at(index, size):
    return pl.ds(pl.multiple_of(index * size, size), size)


def kernel(
    n_ctx, n_head, fast, slow,
    hid, gain, positions, frequency, count, w_qkv, keys, values, w_out,
    out,
    hid_all, w_buf, k_buf, v_buf, wo_buf, ss_own, ss_in, part_q, part_kv, kv_send,
    fast_q, fast_kv, slow_q_out, slow_kv_out, slow_q, slow_kv, kv_own, kv_in,
    q_all, scores, causal, o_own, o_send, st_own,
    of_in, sf_in, os_out, ss_out, os_in, sst_in, a_all, y_mine, y_send, y_in,
    local_sem, hid_sem, sq_sem, rs1_sem, rk1_sem, rs2_sem, rk2_sem, kv_sem, ag1_sem,
    of_sem, sf_sem, os_sem, sst_sem, ag2_sem, y_sem,
):
    c = lax.axis_index("ctx")
    h = lax.axis_index("head")
    z = c // fast
    y = c % fast
    rows = hid.shape[0]
    total = rows * n_head
    own = total // n_ctx
    band = own * fast
    depth = hid.shape[1]
    width = w_buf.shape[1]
    groups = k_buf.shape[0]
    key_rows = keys.shape[0]
    heads = groups * GROUP
    sends = []

    def remote(src, dst, sems, slot, axis, peer):
        return pltpu.make_async_remote_copy(
            src_ref=src, dst_ref=dst,
            send_sem=sems.at[(0,) + slot], recv_sem=sems.at[(1,) + slot],
            device_id={axis: peer}, device_id_type=MESH,
        )

    def send(*args):
        copy = remote(*args)
        copy.start()
        sends.append(copy)
        return copy

    locals_ = [
        pltpu.make_async_copy(w_qkv.at[:, pl.ds(pl.multiple_of(h * width, width), width)], w_buf, local_sem.at[0])
    ]
    for g in range(groups):
        cols = pl.ds(g * HEAD_DIM, HEAD_DIM)
        locals_.append(
            pltpu.make_async_copy(keys.at[:, cols], k_buf.at[g, pl.ds(0, key_rows)], local_sem.at[2 + 2 * g])
        )
        locals_.append(
            pltpu.make_async_copy(
                values.at[:, cols], v_buf.at[g, pl.ds(0, key_rows), pl.ds(0, HEAD_DIM)], local_sem.at[3 + 2 * g]
            )
        )
    locals_.append(pltpu.make_async_copy(w_out, wo_buf, local_sem.at[1]))

    barrier = pltpu.get_barrier_semaphore()
    for k in range(1, n_ctx):
        pl.semaphore_signal(barrier, inc=1, device_id={"ctx": (c + k) % n_ctx}, device_id_type=MESH)
    for k in range(1, n_head):
        pl.semaphore_signal(barrier, inc=1, device_id={"head": (h + k) % n_head}, device_id_type=MESH)
    locals_[0].start()
    my_rows = rows_at(h, rows)
    my_chunk = rows_at(c, own)
    hid_all[my_rows, :] = hid[...]
    v_buf[:, :, HEAD_DIM:] = jnp.ones((groups, key_rows + total, HEAD_DIM), BF16)
    k_buf[:, pl.ds(key_rows, total), :] = jnp.zeros((groups, total, HEAD_DIM), BF16)
    v_buf[:, pl.ds(key_rows, total), pl.ds(0, HEAD_DIM)] = jnp.zeros((groups, total, HEAD_DIM), BF16)
    pl.semaphore_wait(barrier, n_head + n_ctx - 2)

    gathers = [
        send(hid, hid_all.at[my_rows], hid_sem, (k - 1,), "head", (h + k) % n_head) for k in range(1, n_head)
    ]
    for copy in locals_[1:]:
        copy.start()
    for copy in gathers:
        copy.wait_recv()

    features = hid_all[...].astype(F32)
    scaled = (features * gain[...]).astype(BF16)
    contract = (((1,), (1,)), ((), ()))
    locals_[0].wait()
    for g in range(groups):
        base = g * SLOTS * HEAD_DIM
        span = GROUP * HEAD_DIM
        part_q[:, g * span : (g + 1) * span] = jnp.dot(
            scaled, w_buf[:, base : base + span], preferred_element_type=F32
        )
        block = jnp.dot(
            scaled, w_buf[:, base + span : base + SLOTS * HEAD_DIM], preferred_element_type=F32
        )
        part_kv[:, g * 256 : (g + 1) * 256] = block
        kv_send[:, g * 256 : (g + 1) * 256] = block.astype(BF16)

    order = list(range(1, slow)) + [0]
    firsts = {}
    for k in order:
        for j in range(1, fast):
            peer_y = (y + j) % fast
            chunk_rows = rows_at(((z + k) % slow) * fast + peer_y, own)
            peer = z * fast + peer_y
            firsts[j, k] = (
                send(part_q.at[chunk_rows], fast_q.at[j - 1, k], rs1_sem, (j - 1, k), "ctx", peer),
                send(kv_send.at[chunk_rows], fast_kv.at[j - 1, k], rk1_sem, (j - 1, k), "ctx", peer),
            )
    squares = features * features
    high = squares.astype(BF16)
    low = (squares - high.astype(F32)).astype(BF16)
    ones = jnp.ones((8, depth), BF16)
    ss_own[...] = lax.dot_general(ones, high, contract, preferred_element_type=F32) + lax.dot_general(
        ones, low, contract, preferred_element_type=F32
    )
    squares_in = [
        send(ss_own, ss_in.at[k - 1], sq_sem, (k - 1,), "ctx", (c + k) % n_ctx) for k in range(1, n_ctx)
    ]
    picked = lax.broadcasted_iota(jnp.int32, (own, total), 1) == (
        lax.broadcasted_iota(jnp.int32, (own, total), 0) + c * own
    )
    angles = (
        jnp.sum(jnp.where(picked, positions[...].astype(F32), 0.0), axis=1, keepdims=True) * frequency[...]
    )
    cosine = jnp.cos(angles)
    sine = jnp.sin(angles)
    sine = jnp.where(lax.broadcasted_iota(jnp.int32, sine.shape, 1) < HEAD_DIM // 2, -sine, sine)
    seconds = []
    for k in order:
        chunk = (z + k) % slow
        chunk_rows = rows_at(chunk * fast + y, own)
        block_q = part_q[chunk_rows, :]
        block_kv = part_kv[chunk_rows, :]
        for j in range(1, fast):
            for copy in firsts[j, k]:
                copy.wait_recv()
            block_q = block_q + fast_q[j - 1, k]
            block_kv = block_kv + fast_kv[j - 1, k].astype(F32)
        if k:
            slow_q_out[k - 1] = block_q
            slow_kv_out[k - 1] = block_kv.astype(BF16)
            peer = chunk * fast + y
            seconds.append((
                send(slow_q_out.at[k - 1], slow_q.at[k - 1], rs2_sem, (k - 1,), "ctx", peer),
                send(slow_kv_out.at[k - 1], slow_kv.at[k - 1], rk2_sem, (k - 1,), "ctx", peer),
            ))
    for copy in squares_in:
        copy.wait_recv()
    square_total = ss_own[0:1, :]
    for k in range(1, n_ctx):
        square_total = square_total + ss_in[k - 1, 0:1, :]
    square_rows = jnp.sum(jnp.where(picked, square_total, 0.0), axis=1, keepdims=True)
    inv_rms = lax.rsqrt(square_rows / (depth * n_ctx) + 1e-05)
    for k in range(1, slow):
        for copy in seconds[k - 1]:
            copy.wait_recv()
        block_q = block_q + slow_q[k - 1]
        block_kv = block_kv + slow_kv[k - 1].astype(F32)
    block_q = block_q * inv_rms
    block_kv = block_kv * inv_rms

    def turn(entry):
        return entry * cosine + pltpu.roll(entry, HEAD_DIM // 2, 1) * sine

    for g in range(groups):
        at = g * 2 * HEAD_DIM
        kv_own[:, pl.ds(at, HEAD_DIM)] = turn(block_kv[:, at : at + HEAD_DIM]).astype(BF16)
        kv_own[:, pl.ds(at + HEAD_DIM, HEAD_DIM)] = block_kv[:, at + HEAD_DIM : at + 2 * HEAD_DIM].astype(BF16)

    @pl.when(c != 0)
    def _():
        remote(kv_own, kv_in.at[c - 1], kv_sem, (c - 1,), "ctx", 0).start()

    for i in range(heads):
        at = i * HEAD_DIM
        q_all[my_chunk, pl.ds(at, HEAD_DIM)] = turn(block_q[:, at : at + HEAD_DIM]).astype(BF16)

    arrivals = {}
    for k in range(slow):
        for j in range(fast):
            if k or j:
                peer = ((z + k) % slow) * fast + (y + j) % fast
                arrivals[j, k] = send(q_all.at[my_chunk], q_all.at[my_chunk], ag1_sem, (j, k), "ctx", peer)

    for copy in locals_[1:-1]:
        copy.wait()

    @pl.when(c == 0)
    def _():
        for p in range(n_ctx):
            if p:
                remote(kv_own, kv_in.at[p - 1], kv_sem, (p - 1,), "ctx", 1).wait_recv()
            source = kv_in.at[p - 1] if p else kv_own
            at_rows = pl.ds(key_rows + p * own, own)
            for g in range(groups):
                k_buf[g, at_rows, :] = source[:, pl.ds(g * 2 * HEAD_DIM, HEAD_DIM)]
                v_buf[g, at_rows, pl.ds(0, HEAD_DIM)] = source[:, pl.ds((g * 2 + 1) * HEAD_DIM, HEAD_DIM)]

    rate = math.log2(math.e) / math.sqrt(HEAD_DIM)
    key_step = 512
    valid = count[0]
    lanes = lax.broadcasted_iota(jnp.int32, (band, 128), 1)
    spans = [(start, key_step) for start in range(0, key_rows, key_step)] + [(key_rows, total)]
    own_lanes = lax.broadcasted_iota(jnp.int32, (own, 128), 1)

    def head_cols(i):
        return pl.ds(pl.multiple_of(i * HEAD_DIM, HEAD_DIM), HEAD_DIM)

    def attend(band_rows):
        def one_group(g, stats):
            query = jnp.concatenate([q_all[band_rows, head_cols(g * GROUP + i)] for i in range(GROUP)], axis=0)
            top = None
            for start, size in spans:
                score = lax.dot_general(
                    query, k_buf[g, pl.ds(start, size), :], contract, preferred_element_type=F32
                )
                if start == key_rows:
                    score = score + causal[...]
                elif start + size > key_rows // 2:
                    ids = start + lax.broadcasted_iota(jnp.int32, (1, size), 1)
                    score = score + jnp.where(ids < valid, 0.0, NEG_FILL)
                scores[:, pl.ds(start, size)] = score
                for lane in range(0, size, 128):
                    piece = score[:, lane : lane + 128]
                    top = piece if top is None else jnp.maximum(top, piece)
            peak = jnp.max(top, axis=1, keepdims=True)
            sums = jnp.zeros((GROUP * band, 2 * HEAD_DIM), F32)
            for start, size in spans:
                weight = jnp.exp2((scores[:, pl.ds(start, size)] - peak) * rate).astype(BF16)
                sums = sums + jnp.dot(weight, v_buf[g, pl.ds(start, size), :], preferred_element_type=F32)
            for i in range(GROUP):
                part = sums[i * band : (i + 1) * band]
                index = g * GROUP + i
                o_own[band_rows, head_cols(index)] = part[:, :HEAD_DIM]
                o_send[band_rows, head_cols(index)] = part[:, :HEAD_DIM].astype(BF16)
                stats = jnp.where(lanes == index, peak[i * band : (i + 1) * band], stats)
                stats = jnp.where(lanes == 64 + index, part[:, HEAD_DIM:], stats)
            return stats

        st_own[band_rows, :] = lax.fori_loop(0, groups, one_group, jnp.zeros((band, 128), F32))

    def merge(parts):
        top = parts[0][1]
        for _, stat in parts[1:]:
            top = jnp.maximum(top, stat)
        factors = [jnp.exp2((stat - top) * rate) for _, stat in parts]
        sums = None
        for (_, stat), factor in zip(parts, factors):
            term = stat * pltpu.roll(factor, 64, 1)
            sums = term if sums is None else sums + term
        outs = []
        for i in range(heads):
            acc = None
            for (load, _), factor in zip(parts, factors):
                term = load(i) * factor[:, i : i + 1]
                acc = term if acc is None else acc + term
            outs.append(acc)
        return outs, jnp.where(own_lanes < 64, top, sums)

    def cols_of(ref, *index):
        return lambda i: ref[index + (slice(None), pl.ds(i * HEAD_DIM, HEAD_DIM))].astype(F32)

    merged, first_legs, second_legs = {}, {}, {}

    def near_parts(k):
        chunk_rows = rows_at(((z + slow - k) % slow) * fast + y, own)
        parts = [
            (lambda i, at=chunk_rows: o_own[at, pl.ds(i * HEAD_DIM, HEAD_DIM)], st_own[chunk_rows, :])
        ]
        for j in range(1, fast):
            for copy in first_legs[j, k]:
                copy.wait_recv()
            parts.append((cols_of(of_in, j - 1, k), sf_in[j - 1, k]))
        return parts

    def pass_on(k):
        outs, stat = merge(near_parts(k))
        ss_out[k - 1] = stat
        for i in range(heads):
            os_out[k - 1, :, pl.ds(i * HEAD_DIM, HEAD_DIM)] = outs[i].astype(BF16)
        peer = ((z + slow - k) % slow) * fast + y
        second_legs[k] = (
            send(ss_out.at[k - 1], sst_in.at[k - 1], sst_sem, (k - 1,), "ctx", peer),
            send(os_out.at[k - 1], os_in.at[k - 1], os_sem, (k - 1,), "ctx", peer),
        )

    for k in range(slow):
        band_z = (z + slow - k) % slow
        bias = jnp.where(
            lax.broadcasted_iota(jnp.int32, (band, total), 1)
            <= lax.broadcasted_iota(jnp.int32, (band, total), 0) + band_z * band,
            jnp.where(c == 0, 0.0, NEG_FILL),
            NEG_FILL,
        )
        for i in range(GROUP):
            causal[pl.ds(i * band, band), :] = bias
        for j in range(fast):
            if k or j:
                arrivals[j, k].wait_recv()
        attend(rows_at(band_z, band))
        for j in range(1, fast):
            peer_y = (y + j) % fast
            chunk_rows = rows_at(band_z * fast + peer_y, own)
            peer = z * fast + peer_y
            first_legs[j, k] = (
                send(st_own.at[chunk_rows], sf_in.at[j - 1, k], sf_sem, (j - 1, k), "ctx", peer),
                send(o_send.at[chunk_rows], of_in.at[j - 1, k], of_sem, (j - 1, k), "ctx", peer),
            )
        if k >= 2:
            pass_on(k - 1)
    pass_on(slow - 1)
    parts = near_parts(0)
    for k in range(1, slow):
        for copy in second_legs[k]:
            copy.wait_recv()
        parts.append((cols_of(os_in, k - 1), sst_in[k - 1]))
    final, stat = merge(parts)
    for i in range(heads):
        a_all[my_chunk, pl.ds(i * HEAD_DIM, HEAD_DIM)] = (final[i] / stat[:, 64 + i : 65 + i]).astype(BF16)

    across = [
        send(a_all.at[my_chunk], a_all.at[my_chunk], ag2_sem, (0, k), "ctx", ((z + k) % slow) * fast + y)
        for k in range(1, slow)
    ]
    along = {
        (j, 0): send(a_all.at[my_chunk], a_all.at[my_chunk], ag2_sem, (j, 0), "ctx", z * fast + (y + j) % fast)
        for j in range(1, fast)
    }
    locals_[-1].wait()
    per_band = band // rows

    def project(k):
        for j in range(1, fast):
            along[j, k].wait_recv()
        band_z = (z + slow - k) % slow
        result = jnp.dot(a_all[rows_at(band_z, band), :], wo_buf[...], preferred_element_type=F32)
        for i in range(per_band):
            target = band_z * per_band + i
            share = result[i * rows : (i + 1) * rows]
            y_send[rows_at(target, rows), :] = share.astype(BF16)

            @pl.when(target == h)
            def _():
                y_mine[...] = share

            @pl.when(target != h)
            def _():
                slot = (target + n_head - h) % n_head - 1
                remote(
                    y_send.at[rows_at(target, rows)], y_in.at[slot], y_sem, (slot,), "head", target
                ).start()

    for k in range(1, slow):
        across[k - 1].wait_recv()
        block_rows = rows_at(((z + slow - k) % slow) * fast + y, own)
        for j in range(1, fast):
            along[j, k] = send(
                a_all.at[block_rows], a_all.at[block_rows], ag2_sem, (j, k), "ctx", z * fast + (y + j) % fast
            )
        project(k - 1)
    project(slow - 1)
    mine = y_mine[...]
    for k in range(1, n_head):
        target = (h + k) % n_head
        copy = remote(y_send.at[rows_at(target, rows)], y_in.at[k - 1], y_sem, (k - 1,), "head", target)
        copy.wait_recv()
        mine = mine + y_in[k - 1].astype(F32)
        copy.wait_send()
    out[...] = mine.astype(out.dtype)
    for copy in sends:
        copy.wait_send()

    @pl.when(c != 0)
    def _():
        remote(kv_own, kv_in.at[c - 1], kv_sem, (c - 1,), "ctx", 0).wait_send()


def per_device(n_ctx, n_head, hidden, norm_gain, w_qkv, positions, cache_keys, cache_values, key_counts, w_out):
    fast = 2 if n_ctx <= 8 else 8
    slow = n_ctx // fast
    rows, depth = hidden.shape
    total = rows * n_head
    own = total // n_ctx
    groups = KV_HEADS // n_head
    width = groups * SLOTS * HEAD_DIM
    wide = groups * GROUP * HEAD_DIM
    key_rows = cache_keys.shape[0]
    band = own * fast
    thin = groups * 2 * HEAD_DIM
    half = HEAD_DIM // 2
    frequency = np.float32(500000.0) ** (-(np.arange(half, dtype=np.float32) * 2.0 / HEAD_DIM)).astype(np.float32)
    frequency = jnp.asarray(np.concatenate([frequency, frequency])[None, :])
    vmem = pl.BlockSpec(memory_space=pltpu.VMEM)
    hbm = pl.BlockSpec(memory_space=pl.ANY)
    dma = pltpu.SemaphoreType.DMA
    return pl.pallas_call(
        functools.partial(kernel, n_ctx, n_head, fast, slow),
        out_shape=jax.ShapeDtypeStruct((rows, w_out.shape[1]), BF16),
        in_specs=[vmem, vmem, vmem, vmem, pl.BlockSpec(memory_space=pltpu.SMEM), hbm, hbm, hbm, hbm],
        out_specs=vmem,
        scratch_shapes=[
            pltpu.VMEM((total, depth), BF16),
            pltpu.VMEM((depth, width), BF16),
            pltpu.VMEM((groups, key_rows + total, HEAD_DIM), BF16),
            pltpu.VMEM((groups, key_rows + total, 2 * HEAD_DIM), BF16),
            pltpu.VMEM(w_out.shape, BF16),
            pltpu.VMEM((8, total), F32),
            pltpu.VMEM((n_ctx - 1, 8, total), F32),
            pltpu.VMEM((total, wide), F32),
            pltpu.VMEM((total, thin), F32),
            pltpu.VMEM((total, thin), BF16),
            pltpu.VMEM((fast - 1, slow, own, wide), F32),
            pltpu.VMEM((fast - 1, slow, own, thin), BF16),
            pltpu.VMEM((slow - 1, own, wide), F32),
            pltpu.VMEM((slow - 1, own, thin), BF16),
            pltpu.VMEM((slow - 1, own, wide), F32),
            pltpu.VMEM((slow - 1, own, thin), BF16),
            pltpu.VMEM((own, thin), BF16),
            pltpu.VMEM((n_ctx - 1, own, thin), BF16),
            pltpu.VMEM((total, wide), BF16),
            pltpu.VMEM((GROUP * band, key_rows + total), F32),
            pltpu.VMEM((GROUP * band, total), F32),
            pltpu.VMEM((total, wide), F32),
            pltpu.VMEM((total, wide), BF16),
            pltpu.VMEM((total, 128), F32),
            pltpu.VMEM((fast - 1, slow, own, wide), BF16),
            pltpu.VMEM((fast - 1, slow, own, 128), F32),
            pltpu.VMEM((slow - 1, own, wide), BF16),
            pltpu.VMEM((slow - 1, own, 128), F32),
            pltpu.VMEM((slow - 1, own, wide), BF16),
            pltpu.VMEM((slow - 1, own, 128), F32),
            pltpu.VMEM((total, wide), BF16),
            pltpu.VMEM((rows, w_out.shape[1]), F32),
            pltpu.VMEM((total, w_out.shape[1]), BF16),
            pltpu.VMEM((n_head - 1, rows, w_out.shape[1]), BF16),
            dma((2 + 2 * groups,)),
            dma((2, n_head - 1)),
            dma((2, n_ctx - 1)),
            dma((2, fast - 1, slow)),
            dma((2, fast - 1, slow)),
            dma((2, slow - 1)),
            dma((2, slow - 1)),
            dma((2, n_ctx - 1)),
            dma((2, fast, slow)),
            dma((2, fast - 1, slow)),
            dma((2, fast - 1, slow)),
            dma((2, slow - 1)),
            dma((2, slow - 1)),
            dma((2, fast, slow)),
            dma((2, n_head - 1)),
        ],
        compiler_params=pltpu.CompilerParams(
            collective_id=0, has_side_effects=True, vmem_limit_bytes=60 * 1024 * 1024
        ),
    )(hidden, norm_gain.reshape(1, depth), positions.reshape(1, total), frequency, key_counts, w_qkv, cache_keys, cache_values, w_out)


def solution(mesh):
    return jax.shard_map(
        functools.partial(per_device, mesh.shape["ctx"], mesh.shape["head"]),
        mesh=mesh,
        in_specs=(
            P("head", "ctx"),
            P("ctx"),
            P("ctx", None),
            P(),
            P("ctx", "head"),
            P("ctx", "head"),
            P("ctx"),
            P("head", "ctx"),
        ),
        out_specs=P("head", "ctx"),
        check_vma=False,
    )
```

```python
import functools
import math

import jax
import jax.numpy as jnp
import numpy as np
from jax import lax
from jax.experimental import pallas as pl
from jax.experimental.pallas import tpu as pltpu
from jax.sharding import PartitionSpec as P

HEADS = 32
KV_HEADS = 8
HEAD_DIM = 128
GROUP = HEADS // KV_HEADS
SLOTS = GROUP + 2
NEG_FILL = -1e30
MESH = pl.DeviceIdType.MESH
F32 = jnp.float32
BF16 = jnp.bfloat16


def rows_at(index, size):
    return pl.ds(pl.multiple_of(index * size, size), size)


def kernel(
    n_ctx, n_head, fast, slow,
    hid, gain, positions, frequency, count, w_qkv, keys, values, w_out,
    out,
    hid_all, w_buf, k_buf, v_buf, wo_buf, ss_own, ss_in, part_q, part_kv, kv_send,
    fast_q, fast_kv, slow_q_out, slow_kv_out, slow_q, slow_kv, kv_own, kv_in,
    q_all, scores, causal, o_own, o_send, st_own,
    of_in, sf_in, os_out, ss_out, os_in, sst_in, a_all, y_mine, y_send, y_in,
    local_sem, hid_sem, sq_sem, rs1_sem, rk1_sem, rs2_sem, rk2_sem, kv_sem, ag1_sem,
    of_sem, sf_sem, os_sem, sst_sem, ag2_sem, y_sem,
):
    c = lax.axis_index("ctx")
    h = lax.axis_index("head")
    z = c // fast
    y = c % fast
    rows = hid.shape[0]
    total = rows * n_head
    own = total // n_ctx
    band = own * fast
    depth = hid.shape[1]
    width = w_buf.shape[1]
    groups = k_buf.shape[0]
    key_rows = keys.shape[0]
    heads = groups * GROUP
    sends = []

    def remote(src, dst, sems, slot, axis, peer):
        return pltpu.make_async_remote_copy(
            src_ref=src, dst_ref=dst,
            send_sem=sems.at[(0,) + slot], recv_sem=sems.at[(1,) + slot],
            device_id={axis: peer}, device_id_type=MESH,
        )

    def send(*args):
        copy = remote(*args)
        copy.start()
        sends.append(copy)
        return copy

    locals_ = [
        pltpu.make_async_copy(w_qkv.at[:, pl.ds(pl.multiple_of(h * width, width), width)], w_buf, local_sem.at[0])
    ]
    for g in range(groups):
        cols = pl.ds(g * HEAD_DIM, HEAD_DIM)
        locals_.append(
            pltpu.make_async_copy(keys.at[:, cols], k_buf.at[g, pl.ds(0, key_rows)], local_sem.at[2 + 2 * g])
        )
        locals_.append(
            pltpu.make_async_copy(
                values.at[:, cols], v_buf.at[g, pl.ds(0, key_rows), pl.ds(0, HEAD_DIM)], local_sem.at[3 + 2 * g]
            )
        )
    locals_.append(pltpu.make_async_copy(w_out, wo_buf, local_sem.at[1]))

    barrier = pltpu.get_barrier_semaphore()
    for k in range(1, n_ctx):
        pl.semaphore_signal(barrier, inc=1, device_id={"ctx": (c + k) % n_ctx}, device_id_type=MESH)
    for k in range(1, n_head):
        pl.semaphore_signal(barrier, inc=1, device_id={"head": (h + k) % n_head}, device_id_type=MESH)
    locals_[0].start()
    my_rows = rows_at(h, rows)
    my_chunk = rows_at(c, own)
    hid_all[my_rows, :] = hid[...]
    v_buf[:, :, HEAD_DIM:] = jnp.ones((groups, key_rows + total, HEAD_DIM), BF16)
    k_buf[:, pl.ds(key_rows, total), :] = jnp.zeros((groups, total, HEAD_DIM), BF16)
    v_buf[:, pl.ds(key_rows, total), pl.ds(0, HEAD_DIM)] = jnp.zeros((groups, total, HEAD_DIM), BF16)
    pl.semaphore_wait(barrier, n_head + n_ctx - 2)

    gathers = [
        send(hid, hid_all.at[my_rows], hid_sem, (k - 1,), "head", (h + k) % n_head) for k in range(1, n_head)
    ]
    for copy in locals_[1:]:
        copy.start()
    for copy in gathers:
        copy.wait_recv()

    features = hid_all[...].astype(F32)
    scaled = (features * gain[...]).astype(BF16)
    contract = (((1,), (1,)), ((), ()))
    locals_[0].wait()
    for g in range(groups):
        base = g * SLOTS * HEAD_DIM
        span = GROUP * HEAD_DIM
        part_q[:, g * span : (g + 1) * span] = jnp.dot(
            scaled, w_buf[:, base : base + span], preferred_element_type=F32
        )
        block = jnp.dot(
            scaled, w_buf[:, base + span : base + SLOTS * HEAD_DIM], preferred_element_type=F32
        )
        part_kv[:, g * 256 : (g + 1) * 256] = block
        kv_send[:, g * 256 : (g + 1) * 256] = block.astype(BF16)

    order = list(range(1, slow)) + [0]
    firsts = {}
    for k in order:
        for j in range(1, fast):
            peer_y = (y + j) % fast
            chunk_rows = rows_at(((z + k) % slow) * fast + peer_y, own)
            peer = z * fast + peer_y
            firsts[j, k] = (
                send(part_q.at[chunk_rows], fast_q.at[j - 1, k], rs1_sem, (j - 1, k), "ctx", peer),
                send(kv_send.at[chunk_rows], fast_kv.at[j - 1, k], rk1_sem, (j - 1, k), "ctx", peer),
            )
    squares = features * features
    high = squares.astype(BF16)
    low = (squares - high.astype(F32)).astype(BF16)
    ones = jnp.ones((8, depth), BF16)
    ss_own[...] = lax.dot_general(ones, high, contract, preferred_element_type=F32) + lax.dot_general(
        ones, low, contract, preferred_element_type=F32
    )
    squares_in = [
        send(ss_own, ss_in.at[k - 1], sq_sem, (k - 1,), "ctx", (c + k) % n_ctx) for k in range(1, n_ctx)
    ]
    picked = lax.broadcasted_iota(jnp.int32, (own, total), 1) == (
        lax.broadcasted_iota(jnp.int32, (own, total), 0) + c * own
    )
    angles = (
        jnp.sum(jnp.where(picked, positions[...].astype(F32), 0.0), axis=1, keepdims=True) * frequency[...]
    )
    cosine = jnp.cos(angles)
    sine = jnp.sin(angles)
    sine = jnp.where(lax.broadcasted_iota(jnp.int32, sine.shape, 1) < HEAD_DIM // 2, -sine, sine)
    seconds = []
    for k in order:
        chunk = (z + k) % slow
        chunk_rows = rows_at(chunk * fast + y, own)
        block_q = part_q[chunk_rows, :]
        block_kv = part_kv[chunk_rows, :]
        for j in range(1, fast):
            for copy in firsts[j, k]:
                copy.wait_recv()
            block_q = block_q + fast_q[j - 1, k]
            block_kv = block_kv + fast_kv[j - 1, k].astype(F32)
        if k:
            slow_q_out[k - 1] = block_q
            slow_kv_out[k - 1] = block_kv.astype(BF16)
            peer = chunk * fast + y
            seconds.append((
                send(slow_q_out.at[k - 1], slow_q.at[k - 1], rs2_sem, (k - 1,), "ctx", peer),
                send(slow_kv_out.at[k - 1], slow_kv.at[k - 1], rk2_sem, (k - 1,), "ctx", peer),
            ))
    for copy in squares_in:
        copy.wait_recv()
    square_total = ss_own[0:1, :]
    for k in range(1, n_ctx):
        square_total = square_total + ss_in[k - 1, 0:1, :]
    square_rows = jnp.sum(jnp.where(picked, square_total, 0.0), axis=1, keepdims=True)
    inv_rms = lax.rsqrt(square_rows / (depth * n_ctx) + 1e-05)
    for k in range(1, slow):
        for copy in seconds[k - 1]:
            copy.wait_recv()
        block_q = block_q + slow_q[k - 1]
        block_kv = block_kv + slow_kv[k - 1].astype(F32)
    block_q = block_q * inv_rms
    block_kv = block_kv * inv_rms

    def turn(entry):
        return entry * cosine + pltpu.roll(entry, HEAD_DIM // 2, 1) * sine

    for g in range(groups):
        at = g * 2 * HEAD_DIM
        kv_own[:, pl.ds(at, HEAD_DIM)] = turn(block_kv[:, at : at + HEAD_DIM]).astype(BF16)
        kv_own[:, pl.ds(at + HEAD_DIM, HEAD_DIM)] = block_kv[:, at + HEAD_DIM : at + 2 * HEAD_DIM].astype(BF16)

    @pl.when(c != 0)
    def _():
        remote(kv_own, kv_in.at[c - 1], kv_sem, (c - 1,), "ctx", 0).start()

    for i in range(heads):
        at = i * HEAD_DIM
        q_all[my_chunk, pl.ds(at, HEAD_DIM)] = turn(block_q[:, at : at + HEAD_DIM]).astype(BF16)

    arrivals = {}
    for k in order:
        for j in range(fast):
            if k or j:
                peer = ((z + k) % slow) * fast + (y + j) % fast
                arrivals[j, k] = send(q_all.at[my_chunk], q_all.at[my_chunk], ag1_sem, (j, k), "ctx", peer)

    for copy in locals_[1:-1]:
        copy.wait()

    @pl.when(c == 0)
    def _():
        for p in range(n_ctx):
            if p:
                remote(kv_own, kv_in.at[p - 1], kv_sem, (p - 1,), "ctx", 1).wait_recv()
            source = kv_in.at[p - 1] if p else kv_own
            at_rows = pl.ds(key_rows + p * own, own)
            for g in range(groups):
                k_buf[g, at_rows, :] = source[:, pl.ds(g * 2 * HEAD_DIM, HEAD_DIM)]
                v_buf[g, at_rows, pl.ds(0, HEAD_DIM)] = source[:, pl.ds((g * 2 + 1) * HEAD_DIM, HEAD_DIM)]

    rate = math.log2(math.e) / math.sqrt(HEAD_DIM)
    key_step = 512
    valid = count[0]
    lanes = lax.broadcasted_iota(jnp.int32, (band, 128), 1)
    spans = [(start, key_step) for start in range(0, key_rows, key_step)] + [(key_rows, total)]
    own_lanes = lax.broadcasted_iota(jnp.int32, (own, 128), 1)

    def head_cols(i):
        return pl.ds(i * HEAD_DIM, HEAD_DIM)

    def attend(band_rows, between):
        def one_group(g, stats):
            query = jnp.concatenate([q_all[band_rows, head_cols(g * GROUP + i)] for i in range(GROUP)], axis=0)
            top = None
            for start, size in spans:
                score = lax.dot_general(
                    query, k_buf[g, pl.ds(start, size), :], contract, preferred_element_type=F32
                )
                if start == key_rows:
                    score = score + causal[...]
                elif start + size > key_rows // 2:
                    ids = start + lax.broadcasted_iota(jnp.int32, (1, size), 1)
                    score = score + jnp.where(ids < valid, 0.0, NEG_FILL)
                scores[g, :, pl.ds(start, size)] = score
                for lane in range(0, size, 128):
                    piece = score[:, lane : lane + 128]
                    top = piece if top is None else jnp.maximum(top, piece)
            peak = jnp.max(top, axis=1, keepdims=True)
            sums = jnp.zeros((GROUP * band, 2 * HEAD_DIM), F32)
            for start, size in spans:
                weight = jnp.exp2((scores[g, :, pl.ds(start, size)] - peak) * rate).astype(BF16)
                sums = sums + jnp.dot(weight, v_buf[g, pl.ds(start, size), :], preferred_element_type=F32)
            for i in range(GROUP):
                part = sums[i * band : (i + 1) * band]
                index = g * GROUP + i
                o_own[band_rows, head_cols(index)] = part[:, :HEAD_DIM]
                o_send[band_rows, head_cols(index)] = part[:, :HEAD_DIM].astype(BF16)
                stats = jnp.where(lanes == index, peak[i * band : (i + 1) * band], stats)
                stats = jnp.where(lanes == 64 + index, part[:, HEAD_DIM:], stats)
            return stats

        stats = jnp.zeros((band, 128), F32)
        for g in range(groups):
            stats = one_group(g, stats)
            if between is not None and g == 0:
                pass_on(between)
        st_own[band_rows, :] = stats

    def merge(parts):
        top = parts[0][1]
        for _, stat in parts[1:]:
            top = jnp.maximum(top, stat)
        factors = [jnp.exp2((stat - top) * rate) for _, stat in parts]
        sums = None
        for (_, stat), factor in zip(parts, factors):
            term = stat * pltpu.roll(factor, 64, 1)
            sums = term if sums is None else sums + term
        outs = []
        for i in range(heads):
            acc = None
            for (load, _), factor in zip(parts, factors):
                term = load(i) * factor[:, i : i + 1]
                acc = term if acc is None else acc + term
            outs.append(acc)
        return outs, jnp.where(own_lanes < 64, top, sums)

    def cols_of(ref, *index):
        return lambda i: ref[index + (slice(None), pl.ds(i * HEAD_DIM, HEAD_DIM))].astype(F32)

    merged, first_legs, second_legs = {}, {}, {}

    def near_parts(k):
        chunk_rows = rows_at(((z + slow - k) % slow) * fast + y, own)
        parts = [
            (lambda i, at=chunk_rows: o_own[at, pl.ds(i * HEAD_DIM, HEAD_DIM)], st_own[chunk_rows, :])
        ]
        for j in range(1, fast):
            for copy in first_legs[j, k]:
                copy.wait_recv()
            parts.append((cols_of(of_in, j - 1, k), sf_in[j - 1, k]))
        return parts

    def pass_on(k):
        outs, stat = merge(near_parts(k))
        ss_out[k - 1] = stat
        for i in range(heads):
            os_out[k - 1, :, pl.ds(i * HEAD_DIM, HEAD_DIM)] = outs[i].astype(BF16)
        peer = ((z + slow - k) % slow) * fast + y
        second_legs[k] = (
            send(ss_out.at[k - 1], sst_in.at[k - 1], sst_sem, (k - 1,), "ctx", peer),
            send(os_out.at[k - 1], os_in.at[k - 1], os_sem, (k - 1,), "ctx", peer),
        )

    for k in order:
        band_z = (z + slow - k) % slow
        bias = jnp.where(
            lax.broadcasted_iota(jnp.int32, (band, total), 1)
            <= lax.broadcasted_iota(jnp.int32, (band, total), 0) + band_z * band,
            jnp.where(c == 0, 0.0, NEG_FILL),
            NEG_FILL,
        )
        for i in range(GROUP):
            causal[pl.ds(i * band, band), :] = bias
        for j in range(fast):
            if k or j:
                arrivals[j, k].wait_recv()
        attend(rows_at(band_z, band), None if k else slow - 1)
        for j in range(1, fast):
            peer_y = (y + j) % fast
            chunk_rows = rows_at(band_z * fast + peer_y, own)
            peer = z * fast + peer_y
            first_legs[j, k] = (
                send(st_own.at[chunk_rows], sf_in.at[j - 1, k], sf_sem, (j - 1, k), "ctx", peer),
                send(o_send.at[chunk_rows], of_in.at[j - 1, k], of_sem, (j - 1, k), "ctx", peer),
            )
        if k >= 2:
            pass_on(k - 1)
    parts = near_parts(0)
    for k in range(1, slow):
        for copy in second_legs[k]:
            copy.wait_recv()
        parts.append((cols_of(os_in, k - 1), sst_in[k - 1]))
    final, stat = merge(parts)
    for i in range(heads):
        a_all[my_chunk, pl.ds(i * HEAD_DIM, HEAD_DIM)] = (final[i] / stat[:, 64 + i : 65 + i]).astype(BF16)

    across = [
        send(a_all.at[my_chunk], a_all.at[my_chunk], ag2_sem, (0, k), "ctx", ((z + k) % slow) * fast + y)
        for k in range(1, slow)
    ]
    along = {
        (j, 0): send(a_all.at[my_chunk], a_all.at[my_chunk], ag2_sem, (j, 0), "ctx", z * fast + (y + j) % fast)
        for j in range(1, fast)
    }
    locals_[-1].wait()
    per_band = band // rows

    def project(k):
        for j in range(1, fast):
            along[j, k].wait_recv()
        band_z = (z + slow - k) % slow
        result = jnp.dot(a_all[rows_at(band_z, band), :], wo_buf[...], preferred_element_type=F32)
        for i in range(per_band):
            target = band_z * per_band + i
            share = result[i * rows : (i + 1) * rows]
            y_send[rows_at(target, rows), :] = share.astype(BF16)

            @pl.when(target == h)
            def _():
                y_mine[...] = share

            @pl.when(target != h)
            def _():
                slot = (target + n_head - h) % n_head - 1
                remote(
                    y_send.at[rows_at(target, rows)], y_in.at[slot], y_sem, (slot,), "head", target
                ).start()

    for k in range(1, slow):
        across[k - 1].wait_recv()
        block_rows = rows_at(((z + slow - k) % slow) * fast + y, own)
        for j in range(1, fast):
            along[j, k] = send(
                a_all.at[block_rows], a_all.at[block_rows], ag2_sem, (j, k), "ctx", z * fast + (y + j) % fast
            )
        project(k - 1)
    project(slow - 1)
    mine = y_mine[...]
    for k in range(1, n_head):
        target = (h + k) % n_head
        copy = remote(y_send.at[rows_at(target, rows)], y_in.at[k - 1], y_sem, (k - 1,), "head", target)
        copy.wait_recv()
        mine = mine + y_in[k - 1].astype(F32)
        copy.wait_send()
    out[...] = mine.astype(out.dtype)
    for copy in sends:
        copy.wait_send()

    @pl.when(c != 0)
    def _():
        remote(kv_own, kv_in.at[c - 1], kv_sem, (c - 1,), "ctx", 0).wait_send()


def per_device(n_ctx, n_head, hidden, norm_gain, w_qkv, positions, cache_keys, cache_values, key_counts, w_out):
    fast = 2 if n_ctx <= 8 else 8
    slow = n_ctx // fast
    rows, depth = hidden.shape
    total = rows * n_head
    own = total // n_ctx
    groups = KV_HEADS // n_head
    width = groups * SLOTS * HEAD_DIM
    wide = groups * GROUP * HEAD_DIM
    key_rows = cache_keys.shape[0]
    band = own * fast
    thin = groups * 2 * HEAD_DIM
    half = HEAD_DIM // 2
    frequency = np.float32(500000.0) ** (-(np.arange(half, dtype=np.float32) * 2.0 / HEAD_DIM)).astype(np.float32)
    frequency = jnp.asarray(np.concatenate([frequency, frequency])[None, :])
    vmem = pl.BlockSpec(memory_space=pltpu.VMEM)
    hbm = pl.BlockSpec(memory_space=pl.ANY)
    dma = pltpu.SemaphoreType.DMA
    return pl.pallas_call(
        functools.partial(kernel, n_ctx, n_head, fast, slow),
        out_shape=jax.ShapeDtypeStruct((rows, w_out.shape[1]), BF16),
        in_specs=[vmem, vmem, vmem, vmem, pl.BlockSpec(memory_space=pltpu.SMEM), hbm, hbm, hbm, hbm],
        out_specs=vmem,
        scratch_shapes=[
            pltpu.VMEM((total, depth), BF16),
            pltpu.VMEM((depth, width), BF16),
            pltpu.VMEM((groups, key_rows + total, HEAD_DIM), BF16),
            pltpu.VMEM((groups, key_rows + total, 2 * HEAD_DIM), BF16),
            pltpu.VMEM(w_out.shape, BF16),
            pltpu.VMEM((8, total), F32),
            pltpu.VMEM((n_ctx - 1, 8, total), F32),
            pltpu.VMEM((total, wide), F32),
            pltpu.VMEM((total, thin), F32),
            pltpu.VMEM((total, thin), BF16),
            pltpu.VMEM((fast - 1, slow, own, wide), F32),
            pltpu.VMEM((fast - 1, slow, own, thin), BF16),
            pltpu.VMEM((slow - 1, own, wide), F32),
            pltpu.VMEM((slow - 1, own, thin), BF16),
            pltpu.VMEM((slow - 1, own, wide), F32),
            pltpu.VMEM((slow - 1, own, thin), BF16),
            pltpu.VMEM((own, thin), BF16),
            pltpu.VMEM((n_ctx - 1, own, thin), BF16),
            pltpu.VMEM((total, wide), BF16),
            pltpu.VMEM((groups, GROUP * band, key_rows + total), F32),
            pltpu.VMEM((GROUP * band, total), F32),
            pltpu.VMEM((total, wide), F32),
            pltpu.VMEM((total, wide), BF16),
            pltpu.VMEM((total, 128), F32),
            pltpu.VMEM((fast - 1, slow, own, wide), BF16),
            pltpu.VMEM((fast - 1, slow, own, 128), F32),
            pltpu.VMEM((slow - 1, own, wide), BF16),
            pltpu.VMEM((slow - 1, own, 128), F32),
            pltpu.VMEM((slow - 1, own, wide), BF16),
            pltpu.VMEM((slow - 1, own, 128), F32),
            pltpu.VMEM((total, wide), BF16),
            pltpu.VMEM((rows, w_out.shape[1]), F32),
            pltpu.VMEM((total, w_out.shape[1]), BF16),
            pltpu.VMEM((n_head - 1, rows, w_out.shape[1]), BF16),
            dma((2 + 2 * groups,)),
            dma((2, n_head - 1)),
            dma((2, n_ctx - 1)),
            dma((2, fast - 1, slow)),
            dma((2, fast - 1, slow)),
            dma((2, slow - 1)),
            dma((2, slow - 1)),
            dma((2, n_ctx - 1)),
            dma((2, fast, slow)),
            dma((2, fast - 1, slow)),
            dma((2, fast - 1, slow)),
            dma((2, slow - 1)),
            dma((2, slow - 1)),
            dma((2, fast, slow)),
            dma((2, n_head - 1)),
        ],
        compiler_params=pltpu.CompilerParams(
            collective_id=0, has_side_effects=True, vmem_limit_bytes=60 * 1024 * 1024
        ),
    )(hidden, norm_gain.reshape(1, depth), positions.reshape(1, total), frequency, key_counts, w_qkv, cache_keys, cache_values, w_out)


def solution(mesh):
    return jax.shard_map(
        functools.partial(per_device, mesh.shape["ctx"], mesh.shape["head"]),
        mesh=mesh,
        in_specs=(
            P("head", "ctx"),
            P("ctx"),
            P("ctx", None),
            P(),
            P("ctx", "head"),
            P("ctx", "head"),
            P("ctx"),
            P("head", "ctx"),
        ),
        out_specs=P("head", "ctx"),
        check_vma=False,
    )
```
